1024 devices in a mesh: section: 8 (over y), shard: 128 (over z, x, core).
Axes of the slice: x: 4, y: 8, z: 16, core: 2. Of those that a mesh axis runs over, the one named last changes fastest.
Arguments:
- section_inputs: bfloat16 [8, 2, 384, 16384], P('section', None, None, 'shard'), may hold values from -12 to 12
- top_grad: bfloat16 [2, 384, 16384], P(None, None, 'shard'), may hold values from -6 to 6
- norm_gain: float32 [8, 16384], P('section', 'shard'), may hold values from 0.1 to 1.9
- key_grad: bfloat16 [8, 2, 384, 512], P('section'), may hold values from -18 to 18
- value_grad: bfloat16 [8, 2, 384, 512], P('section'), may hold values from -6 to 6
- key_weight: bfloat16 [8, 512, 16384], P('section', None, 'shard'), may hold values from -0.046875 to 0.046875
- value_weight: bfloat16 [8, 512, 16384], P('section', None, 'shard'), may hold values from -0.046875 to 0.046875
- first_codes: int32 [8, 2, 512, 16384], P('section', None, None, 'shard'), may hold values from 0 to 15
- second_codes: int32 [8, 2, 512, 16384], P('section', None, None, 'shard'), may hold values from 0 to 15
- first_scale: float32 [8, 2, 512, 128], P('section', None, None, 'shard'), may hold values from 1.726335e-05 to 0.00017263349
- second_scale: float32 [8, 2, 512, 128], P('section', None, None, 'shard'), may hold values from 7.4505807e-10 to 7.450581e-09
Outputs:
- direction: float32 [8, 2, 512, 16384], P('section', None, None, 'shard')
- first_ratio: float32 [8, 2, 512, 16384], P('section', None, None, 'shard')
- second_ratio: float32 [8, 2, 512, 16384], P('section', None, None, 'shard')
- leaving: bfloat16 [8, 2, 384, 16384], P('section', None, None, 'shard')
The draws below stay inside these ranges and needn't reach their ends.
Inputs may be any that keep to these rules, and one draw needn't show every extreme that they name: `first_codes`: codes follow the encoding of the steps.
All inputs are finite; a program needn't handle non-finite values. Where the reference program divides by a largest or mean magnitude, that divisor is 1e-20 or more.
Results may differ from the reference program's by a relative error of at most 0.0085.
The reference program's roundings to bfloat16 on the way (of `normed`) count: a program that leaves them out, or rounds other values in their place, can miss the bound.
Values may be sent and summed in bfloat16 or wider, within the bound.
No kernel may reach another device: no remote copies, remote signals or barrier semaphores. Data moves between devices by JAX's collectives and lax.ppermute only.
A program may use at most 32 MiB of HBM per device.

```python
import math
import jax
import jax.numpy as jnp
from jax import lax

D = 16384
TOK = 384
MB = 2
QB = 128
STEP = 20
KVW = 512
N_SECTION = 8


def joint_draw(key):
    keys = jax.random.split(jax.random.fold_in(key, 41), 5)
    shape = (N_SECTION, MB, TOK, D)
    ramp = 1.0 + 2.0 * jnp.arange(N_SECTION, dtype=jnp.float32) / max(N_SECTION - 1, 1)
    keys_grad = jnp.clip(jax.random.normal(keys[0], (N_SECTION, MB, TOK, KVW)) * ramp[:, None, None, None], -18.0, 18.0)
    weight = jnp.clip(jax.random.normal(keys[1], (N_SECTION, KVW, D)), -6.0, 6.0) * D ** (-0.5)

    def project_section(pair):
        return jnp.dot(pair[0].reshape(MB * TOK, KVW), pair[1], precision=lax.Precision.HIGHEST)
    along = lax.map(project_section, (keys_grad, weight)).reshape(shape)
    along = along / ramp[:, None, None, None] * (D / KVW) ** 0.5
    feature = jnp.arange(D, dtype=jnp.float32) / (D - 1)
    column_scale = jnp.exp(jax.random.uniform(keys[2], (D,), minval=math.log(0.3), maxval=0.0)) * (1.0 + 2.0 * feature)
    row_scale = jnp.exp(jax.random.uniform(keys[3], (N_SECTION, MB, TOK, 1), minval=math.log(0.5), maxval=math.log(2.0)))
    noise = jax.random.normal(keys[4], shape)
    inputs = jnp.clip(noise * column_scale * row_scale + 1.5 * along, -12.0, 12.0)
    return (inputs, keys_grad, weight)


def draw_section_inputs(key, part):
    return joint_draw(key)[0].astype(jnp.float32).astype(jnp.bfloat16)


def draw_key_grad(key, part):
    return joint_draw(key)[1].astype(jnp.float32).astype(jnp.bfloat16)


def draw_key_weight(key, part):
    return joint_draw(key)[2].astype(jnp.float32).astype(jnp.bfloat16)


def with_ends(array, stream_key, least, high):
    shape = array.shape
    index_at = [jax.random.randint(jax.random.fold_in(stream_key, axis), (), 0, shape[axis]) for axis in range(len(shape))]
    array = array.at[tuple(index_at)].set(least)
    longest = shape.index(max(shape))
    index_at[longest] = (index_at[longest] + 1) % shape[longest]
    return array.at[tuple(index_at)].set(high)


def block_levels(stream_key, dims, shards, low, largest):
    def one(dim, shards_of):
        steps = jax.random.uniform(jax.random.fold_in(jax.random.fold_in(stream_key, 6), dim), (shards_of,), jnp.float32, low / len(shards), largest / len(shards))
        return jnp.repeat(jnp.exp(steps), dims[dim] // shards_of).reshape((-1,) + (1,) * (len(dims) - dim - 1))

    level = one(*shards[0])
    for cut in shards[1:]:
        level = level * one(*cut)
    return level


def centred(own_key, shape, deviation, reach, shards=(), held_as=jnp.bfloat16):
    drawn = jax.random.normal(own_key, shape, jnp.float32) * deviation
    if len(shards) > 0:
        drawn = block_levels(own_key, shape, shards, -0.22, 0.18) * drawn
    return jnp.clip(drawn, min=-reach, max=reach).astype(held_as)


def setup_inputs(seed: int = 0) -> dict:
    splits = jax.random.split(jax.random.key(seed), 12)
    return {
        "section_inputs": draw_section_inputs(jax.random.fold_in(splits[11], 71), 0),
        "top_grad": centred(splits[1], (MB, TOK, D), 1.0, 6.0, ((2, 128),)),
        "norm_gain": jnp.clip(1.0 + 0.18 * jax.random.normal(splits[2], (N_SECTION, D), jnp.float32), 0.1, 1.9),
        "key_grad": draw_key_grad(jax.random.fold_in(splits[11], 71), 0),
        "value_grad": centred(splits[4], (N_SECTION, MB, TOK, KVW), 1.0, 6.0, ((0, 8),)),
        "key_weight": draw_key_weight(jax.random.fold_in(splits[11], 71), 0),
        "value_weight": centred(splits[6], (N_SECTION, KVW, D), D ** -0.5, 0.046875, ((0, 8), (2, 128))),
        "first_codes": with_ends(jax.random.randint(splits[7], (N_SECTION, 2, KVW, D), 0, 16), jax.random.fold_in(splits[7], 1), 0, 15).astype(jnp.int32),
        "second_codes": with_ends(jax.random.randint(splits[8], (N_SECTION, 2, KVW, D), 0, 16), jax.random.fold_in(splits[8], 1), 0, 15).astype(jnp.int32),
        "first_scale": jnp.clip(jnp.exp(math.log(0.00017263349) - 2.30258503 * jax.random.uniform(splits[9], (N_SECTION, 2, KVW, D // QB), jnp.float32) ** block_levels(splits[9], (N_SECTION, 2, KVW, D // QB), ((0, 8), (3, 128)), -0.2, 0.2)), 1.72633499460062e-05, 0.00017263349),
        "second_scale": jnp.clip(jnp.exp(math.log(7.450580596923828e-09) - 2.3025851 * jax.random.uniform(splits[10], (N_SECTION, 2, KVW, D // QB), jnp.float32) ** block_levels(splits[10], (N_SECTION, 2, KVW, D // QB), ((0, 8), (3, 128)), -0.2, 0.2)), 7.450580707946131e-10, 7.450580596923828e-09),
    }


beta_one = 0.9
beta_two = 0.95
clip_norm = 1.0

def optimizer(gradients, square_total, first_codes, second_codes, first_scale, second_scale):
    clip_factor = jnp.minimum(1.0, clip_norm / (jnp.sqrt(square_total) + 1e-06))
    clipped = clip_factor * gradients
    sign_part = 1.0 - 2.0 * (first_codes // 8).astype(jnp.float32)
    first_old = jnp.repeat(first_scale, QB, axis=-1) * sign_part * jnp.exp2(-(first_codes % 8).astype(jnp.float32))
    second_old = jnp.repeat(second_scale, QB, axis=-1) * jnp.exp2(-second_codes.astype(jnp.float32))
    first_new = beta_one * first_old + (1.0 - beta_one) * clipped
    second_new = beta_two * second_old + (1.0 - beta_two) * clipped * clipped
    bias_one = 1.0 - beta_one ** STEP
    bias_two = 1.0 - beta_two ** STEP
    direction = first_new / bias_one / (jnp.sqrt(second_new / bias_two) + 1e-08)
    blocks = clipped.reshape(clipped.shape[:-1] + (clipped.shape[-1] // QB, QB))
    first_bound = beta_one * first_scale + (1.0 - beta_one) * lax.optimization_barrier(jnp.max(jnp.abs(blocks), axis=-1))
    second_bound = beta_two * second_scale + (1.0 - beta_two) * lax.optimization_barrier(jnp.max(blocks * blocks, axis=-1))
    first_ratio = first_new / jnp.repeat(first_bound, QB, axis=-1)
    second_ratio = second_new / jnp.repeat(second_bound, QB, axis=-1)
    return (direction, first_ratio, second_ratio)

def reference(section_inputs, top_grad, norm_gain, key_grad, value_grad, key_weight, value_weight, first_codes, second_codes, first_scale, second_scale):
    row_count = MB * TOK
    running = top_grad.reshape(row_count, D).astype(jnp.float32)
    leaving_list = [None] * N_SECTION
    grad_list = [None] * N_SECTION
    for section_num in range(N_SECTION - 1, -1, -1):
        inputs = section_inputs[section_num].reshape(row_count, D)
        inputs_f = inputs.astype(jnp.float32)
        keys_rows = key_grad[section_num].reshape(row_count, KVW)
        values_rows = value_grad[section_num].reshape(row_count, KVW)
        gain = norm_gain[section_num]
        d_normed = jnp.dot(keys_rows, key_weight[section_num], preferred_element_type=jnp.float32) + jnp.dot(values_rows, value_weight[section_num], preferred_element_type=jnp.float32)
        power = lax.optimization_barrier(jnp.sum(inputs_f * inputs_f, axis=1))
        root = 1.0 / jnp.sqrt(power / D + 1e-05)
        normed = (inputs_f * root[:, None] * gain).astype(jnp.bfloat16)
        row_dot = lax.optimization_barrier(jnp.sum(inputs_f * gain * d_normed, axis=1))
        input_grad = gain * d_normed * root[:, None] - inputs_f * (root * root * root * row_dot / D)[:, None]
        running = running + input_grad
        leaving_list[section_num] = running.astype(jnp.bfloat16).reshape(MB, TOK, D)
        grad_list[section_num] = jnp.stack([jnp.dot(keys_rows.T, normed, preferred_element_type=jnp.float32), jnp.dot(values_rows.T, normed, preferred_element_type=jnp.float32)])
    gradients = jnp.stack(grad_list)
    square_total = jnp.sum(gradients * gradients)
    direction, first_ratio, second_ratio = optimizer(gradients, square_total, first_codes, second_codes, first_scale, second_scale)
    return (direction, first_ratio, second_ratio, jnp.stack(leaving_list))
```

```python
import jax
import jax.numpy as jnp
from jax import lax
from jax.sharding import Mesh
from jax.sharding import PartitionSpec as P


D = 16384
QB = 128
STEP = 20
SHARD = ("shard_0", "shard_1", "shard_2")


beta_one = 0.9
beta_two = 0.95
clip_norm = 1.0


def gathered_sum(x, axes):
    members = lax.axis_size(axes)
    copies = jnp.broadcast_to(x[None], (members,) + x.shape)
    return jnp.sum(exchange(copies, axes), axis=0)


def exchange(x, axes):
    return lax.all_to_all(x, axes, split_axis=0, concat_axis=0, tiled=True)


def optimizer(gradients, square_total, first_codes, second_codes, first_scale, second_scale):
    clip_factor = jnp.minimum(1.0, clip_norm / (jnp.sqrt(square_total) + 1e-06))
    clipped = clip_factor * gradients
    sign_part = 1.0 - 2.0 * (first_codes // 8).astype(jnp.float32)
    first_old = (
        jnp.repeat(first_scale, QB, axis=-1)
        * sign_part
        * jnp.exp2(-(first_codes % 8).astype(jnp.float32))
    )
    second_old = jnp.repeat(second_scale, QB, axis=-1) * jnp.exp2(-second_codes.astype(jnp.float32))
    first_new = beta_one * first_old + (1.0 - beta_one) * clipped
    second_new = beta_two * second_old + (1.0 - beta_two) * clipped * clipped
    bias_one = 1.0 - beta_one**STEP
    bias_two = 1.0 - beta_two**STEP
    direction = first_new / bias_one / (jnp.sqrt(second_new / bias_two) + 1e-08)
    blocks = clipped.reshape(clipped.shape[:-1] + (clipped.shape[-1] // QB, QB))
    first_bound = beta_one * first_scale + (1.0 - beta_one) * jnp.max(jnp.abs(blocks), axis=-1)
    second_bound = beta_two * second_scale + (1.0 - beta_two) * jnp.max(blocks * blocks, axis=-1)
    first_ratio = first_new / jnp.repeat(first_bound, QB, axis=-1)
    second_ratio = second_new / jnp.repeat(second_bound, QB, axis=-1)
    return (direction, first_ratio, second_ratio)


def project(left, right):
    return lax.dot_general(
        left, right, (((0,), (0,)), ((), ())), preferred_element_type=jnp.float32
    )


def on_device(
    section_inputs,
    top_grad,
    norm_gain,
    key_grad,
    value_grad,
    key_weight,
    value_weight,
    first_codes,
    second_codes,
    first_scale,
    second_scale,
):
    micro_count = top_grad.shape[0]
    token_count = top_grad.shape[1]
    width_local = top_grad.shape[2]
    row_count = micro_count * token_count
    section_count = lax.axis_size("section")
    inputs = section_inputs[0].reshape(row_count, width_local)
    inputs_f = inputs.astype(jnp.float32)
    gain = norm_gain[0]
    keys_rows = key_grad[0].reshape(row_count, key_grad.shape[3])
    values_rows = value_grad[0].reshape(row_count, value_grad.shape[3])
    d_normed = jnp.dot(keys_rows, key_weight[0], preferred_element_type=jnp.float32) + jnp.dot(
        values_rows, value_weight[0], preferred_element_type=jnp.float32
    )
    scaled_grad = gain * d_normed
    local_power = jnp.sum(inputs_f * inputs_f, axis=1)
    local_dot = jnp.sum(inputs_f * scaled_grad, axis=1)
    stats = jnp.stack([local_power, local_dot]).reshape(2 * row_count // 128, 128)
    for axes in (("shard_1", "shard_2"), "shard_0"):
        stats = gathered_sum(stats, axes)
    power, row_dot = stats.reshape(2, row_count)
    root = 1.0 / jnp.sqrt(power / D + 1e-05)
    normed = (inputs_f * root[:, None] * gain).astype(jnp.bfloat16)
    gradients = jnp.stack([project(keys_rows, normed), project(values_rows, normed)])
    square_total = jnp.broadcast_to(jnp.sum(gradients * gradients), (1, 128))
    for axes in ("section", SHARD):
        square_total = gathered_sum(square_total, axes)
    square_total = square_total[0, 0]
    block_rows = row_count // section_count
    input_grad = (
        scaled_grad * root[:, None]
        - inputs_f * (root * root * root * row_dot / D)[:, None]
    )
    split_rows = input_grad.astype(jnp.bfloat16).reshape(
        section_count, block_rows, width_local
    )
    by_section = exchange(split_rows, "section")
    top_rows = lax.dynamic_slice_in_dim(
        top_grad.reshape(row_count, width_local), lax.axis_index("section") * block_rows, block_rows
    )
    running = top_rows.astype(jnp.float32)
    sums = [None] * section_count
    for t in range(section_count - 1, -1, -1):
        running = running + by_section[t].astype(jnp.float32)
        sums[t] = running.astype(jnp.bfloat16)
    suffix = jnp.stack(sums)
    returned = exchange(suffix, "section")
    leaving = returned.reshape(1, micro_count, token_count, width_local)
    direction, first_ratio, second_ratio = optimizer(
        gradients, square_total, first_codes[0], second_codes[0], first_scale[0], second_scale[0]
    )
    return (direction[None], first_ratio[None], second_ratio[None], leaving)


def solution(mesh):
    finer = Mesh(
        mesh.devices.reshape(mesh.shape["section"], 16, 4, 2),
        ("section", "shard_0", "shard_1", "shard_2"),
    )
    in_specs = (
        P("section", None, None, SHARD),
        P(None, None, SHARD),
        P("section", SHARD),
        P("section", None, None, None),
        P("section", None, None, None),
        P("section", None, SHARD),
        P("section", None, SHARD),
        P("section", None, None, SHARD),
        P("section", None, None, SHARD),
        P("section", None, None, SHARD),
        P("section", None, None, SHARD),
    )
    out_specs = (
        P("section", None, None, SHARD),
        P("section", None, None, SHARD),
        P("section", None, None, SHARD),
        P("section", None, None, SHARD),
    )
    return jax.shard_map(
        on_device, mesh=finer, in_specs=in_specs, out_specs=out_specs, check_vma=False
    )
```

```python
import jax
import jax.numpy as jnp
from jax import lax
from jax.experimental import pallas as pl
from jax.experimental.pallas import tpu as pltpu
from jax.sharding import Mesh
from jax.sharding import PartitionSpec as P


D = 16384
STEP = 20
SHARD = ("shard_0", "shard_1", "shard_2")
SIDE = 128
TAIL = 16

beta_one = 0.9
beta_two = 0.95
clip_norm = 1.0

F32 = jnp.float32
BF16 = jnp.bfloat16


def kernel_call(body, out_shape, flops, moved, room=16 * 2**20, **options):
    return pl.pallas_call(
        body,
        out_shape=out_shape,
        compiler_params=pltpu.CompilerParams(vmem_limit_bytes=room),
        cost_estimate=pl.CostEstimate(flops=flops, bytes_accessed=moved, transcendentals=0),
        **options,
    )


def shape(dims, dtype=F32):
    return jax.ShapeDtypeStruct(dims, dtype)


def exchange(x, axes):
    return lax.all_to_all(x, axes, split_axis=0, concat_axis=0, tiled=True)


def turned_column(row):
    return jnp.transpose(jnp.broadcast_to(row, (SIDE, SIDE)))


def stats_body(x, gain, keys, values, key_w, value_w, copies, x_turned, u_turned):
    gain_column = turned_column(gain[...])
    blocks = x.shape[0] // SIDE
    for block in range(blocks):
        rows = pl.ds(block * SIDE, SIDE)
        grad = jnp.dot(keys[rows, :], key_w[...], preferred_element_type=F32)
        grad = grad + jnp.dot(values[rows, :], value_w[...], preferred_element_type=F32)
        x_block = jnp.transpose(x[rows, :].astype(F32))
        u_block = gain_column * jnp.transpose(grad)
        x_turned[:, rows] = x_block.astype(BF16)
        u_turned[:, rows] = u_block
        copies[0, pl.ds(block, 1), :] = jnp.sum(x_block * x_block, axis=0, keepdims=True)
        copies[0, pl.ds(blocks + block, 1), :] = jnp.sum(x_block * u_block, axis=0, keepdims=True)
    own = copies[0]
    for member in range(1, copies.shape[0]):
        copies[member] = own


def spread_body(parts, copies):
    total = parts[0]
    for member in range(1, parts.shape[0]):
        total = total + parts[member]
    copies[...] = jnp.broadcast_to(total[None], copies.shape)


def summed(parts):
    total = parts[0]
    for member in range(1, parts.shape[0]):
        total = total + parts[member]
    return total


def roots(power):
    return 1.0 / jnp.sqrt(power / D + 1e-05)


def gradient_body(
    parts, x_turned, u_turned, gain, keys, values, key_g, value_g, payload, normed
):
    stats = summed(parts)
    blocks = stats.shape[0] // 2
    root = roots(stats[:blocks])
    gain_column = turned_column(gain[...])
    for block in range(blocks):
        rows = pl.ds(block * SIDE, SIDE)
        scaled = x_turned[:, rows].astype(F32) * root[block : block + 1] * gain_column
        normed[:, rows] = scaled.astype(BF16)
    key_g[...] = jnp.dot(normed[...], keys[...], preferred_element_type=F32)
    value_g[...] = jnp.dot(normed[...], values[...], preferred_element_type=F32)
    squares = key_g[...] * key_g[...] + value_g[...] * value_g[...]
    row = jnp.sum(squares, axis=0, keepdims=True)
    lanes = row[:, :SIDE]
    for start in range(SIDE, row.shape[1], SIDE):
        lanes = lanes + row[:, start : start + SIDE]
    factor = root * root * root * stats[blocks:] / D
    sections, padded_rows, width = payload.shape
    block_rows = padded_rows - TAIL
    for block in range(blocks):
        rows = pl.ds(block * SIDE, SIDE)
        grad = (
            u_turned[:, rows] * root[block : block + 1]
            - x_turned[:, rows].astype(F32) * factor[block : block + 1]
        )
        grad = jnp.transpose(grad).astype(BF16)
        done = 0
        while done < SIDE:
            section, offset = divmod(block * SIDE + done, block_rows)
            count = min(SIDE - done, block_rows - offset)
            payload[section, pl.ds(offset, count), :] = grad[done : done + count]
            done += count
    tail = lax.broadcasted_iota(jnp.int32, (TAIL, width), 0)
    high = lanes.astype(BF16).astype(F32)
    middle = (lanes - high).astype(BF16).astype(F32)
    low = lanes - high - middle
    pieces = jnp.where(tail == 0, high, 0.0)
    pieces = jnp.where(tail == 1, middle, pieces)
    pieces = jnp.where(tail == 2, low, pieces).astype(BF16)
    for section in range(sections):
        payload[section, pl.ds(block_rows, TAIL), :] = pieces


def square_spread_body(received, copies):
    start = received.shape[1] - TAIL
    pieces = received[0, pl.ds(start, TAIL), :].astype(F32)
    for member in range(1, received.shape[0]):
        pieces = pieces + received[member, pl.ds(start, TAIL), :].astype(F32)
    lanes = jnp.sum(pieces, axis=0, keepdims=True)
    copies[...] = jnp.broadcast_to(lanes[None], copies.shape)


def suffix_body(by_section, top, out):
    running = top[...].astype(F32)
    for section in range(by_section.shape[0] - 1, -1, -1):
        running = running + by_section[section, pl.ds(0, top.shape[0]), :].astype(F32)
        out[section] = running.astype(BF16)


def first_body(key_g, value_g, codes, scale, grads, old, largest):
    for kind, turned in enumerate((key_g, value_g)):
        largest[kind] = jnp.max(jnp.abs(turned[...]), axis=0, keepdims=True)
        for start in range(0, turned.shape[1], SIDE):
            rows = pl.ds(start, SIDE)
            grads[kind, rows, :] = jnp.transpose(turned[:, rows])
            code = codes[kind, rows, :]
            sign_part = jnp.where(code >= 8, -beta_one, beta_one)
            scales = turned_column(scale[kind, :, rows])
            old[kind, rows, :] = scales * sign_part * jnp.exp2(-(code & 7).astype(F32))


def second_body(codes, scale, old):
    for kind in range(codes.shape[0]):
        for start in range(0, codes.shape[1], SIDE):
            rows = pl.ds(start, SIDE)
            scales = turned_column(beta_two * scale[kind, :, rows])
            old[kind, rows, :] = scales * jnp.exp2(-codes[kind, rows, :].astype(F32))


def adam_body(
    parts, grads, first_old, second_old, first_scale, second_scale, largest, way, first, second
):
    total = jnp.sum(summed(parts), axis=1, keepdims=True)
    clip_factor = jnp.minimum(1.0, clip_norm / (jnp.sqrt(total) + 1e-06))
    bias_one = 1.0 - beta_one**STEP
    bias_two = 1.0 - beta_two**STEP
    edge = clip_factor * largest[0]
    first_part = 1.0 / (beta_one * first_scale[0] + (1.0 - beta_one) * edge)
    second_part = 1.0 / (beta_two * second_scale[0] + (1.0 - beta_two) * edge * edge)
    for start in range(0, grads.shape[1], SIDE):
        rows = pl.ds(start, SIDE)
        clipped = clip_factor * grads[0, rows, :]
        first_new = first_old[0, rows, :] + (1.0 - beta_one) * clipped
        second_new = second_old[0, rows, :] + (1.0 - beta_two) * clipped * clipped
        root = jnp.sqrt(second_new * (1.0 / bias_two)) + 1e-08
        way[0, rows, :] = first_new * (1.0 / bias_one) / root
        first[0, rows, :] = first_new * turned_column(first_part[:, start : start + SIDE])
        second[0, rows, :] = second_new * turned_column(second_part[:, start : start + SIDE])


def on_device(
    section_inputs,
    top_grad,
    norm_gain,
    key_grad,
    value_grad,
    key_weight,
    value_weight,
    first_codes,
    second_codes,
    first_scale,
    second_scale,
):
    micro_count, token_count, width = top_grad.shape
    row_count = micro_count * token_count
    features = key_grad.shape[3]
    sections = lax.axis_size("section")
    block_rows = row_count // sections
    stat_rows = 2 * row_count // SIDE
    x = section_inputs[0].reshape(row_count, width)
    keys = key_grad[0].reshape(row_count, features)
    values = value_grad[0].reshape(row_count, features)
    matmul = 2 * row_count * features * width
    slab = 4 * row_count * width
    moments = (2, features, width)
    moment_bytes = 4 * 2 * features * width

    copies, x_turned, u_turned = kernel_call(
        stats_body,
        (
            shape((lax.axis_size(("shard_1", "shard_2")), stat_rows, SIDE)),
            shape((width, row_count), BF16),
            shape((width, row_count)),
        ),
        2 * matmul,
        4 * slab,
        room=60 * 10**6,
    )(x, norm_gain, keys, values, key_weight[0], value_weight[0])
    parts = exchange(copies, ("shard_1", "shard_2"))
    copies = kernel_call(
        spread_body, shape((lax.axis_size("shard_0"), stat_rows, SIDE)), 2**14, 2**17
    )(parts)
    parts = exchange(copies, "shard_0")

    key_g, value_g, payload = kernel_call(
        gradient_body,
        (
            shape((width, features)),
            shape((width, features)),
            shape((sections, block_rows + TAIL, width), BF16),
        ),
        2 * matmul,
        4 * slab,
        scratch_shapes=[pltpu.VMEM((width, row_count), BF16)],
    )(parts, x_turned, u_turned, norm_gain, keys, values)
    received = exchange(payload, "section")
    copies = kernel_call(
        square_spread_body, shape((lax.axis_size(SHARD), 1, SIDE)), 2**14, 2**17
    )(received)
    squares = exchange(copies, SHARD)

    scale_rows = (2, 1, features)
    first_scales = first_scale.reshape(scale_rows)
    second_scales = second_scale.reshape(scale_rows)
    grads, first_old, largest = kernel_call(
        first_body,
        (shape(moments), shape(moments), shape(scale_rows)),
        moment_bytes,
        4 * moment_bytes,
    )(key_g, value_g, first_codes[0], first_scales)
    second_old = kernel_call(
        second_body, shape(moments), moment_bytes, 2 * moment_bytes
    )(second_codes[0], second_scales)

    top_rows = lax.dynamic_slice_in_dim(
        top_grad.reshape(row_count, width), lax.axis_index("section") * block_rows, block_rows
    )
    suffix = kernel_call(
        suffix_body, shape((sections, block_rows, width), BF16), slab, slab
    )(received, top_rows)
    returned = exchange(suffix, "section")
    leaving = returned.reshape(1, micro_count, token_count, width)

    whole = pl.BlockSpec(squares.shape, lambda kind: (0, 0, 0))
    one = pl.BlockSpec((1,) + moments[1:], lambda kind: (kind, 0, 0))
    row = pl.BlockSpec((1,) + scale_rows[1:], lambda kind: (kind, 0, 0))
    outputs = kernel_call(
        adam_body,
        (shape(moments),) * 3,
        20 * moment_bytes,
        6 * moment_bytes,
        grid=(2,),
        in_specs=[whole] + [one] * 3 + [row] * 3,
        out_specs=[one] * 3,
    )(squares, grads, first_old, second_old, first_scales, second_scales, largest)
    direction, first_ratio, second_ratio = outputs
    return (direction[None], first_ratio[None], second_ratio[None], leaving)


def solution(mesh):
    finer = Mesh(
        mesh.devices.reshape(mesh.shape["section"], 16, 4, 2),
        ("section", "shard_0", "shard_1", "shard_2"),
    )
    in_specs = (
        P("section", None, None, SHARD),
        P(None, None, SHARD),
        P("section", SHARD),
        P("section", None, None, None),
        P("section", None, None, None),
        P("section", None, SHARD),
        P("section", None, SHARD),
        P("section", None, None, SHARD),
        P("section", None, None, SHARD),
        P("section", None, None, SHARD),
        P("section", None, None, SHARD),
    )
    out_specs = (
        P("section", None, None, SHARD),
        P("section", None, None, SHARD),
        P("section", None, None, SHARD),
        P("section", None, None, SHARD),
    )
    return jax.shard_map(
        on_device, mesh=finer, in_specs=in_specs, out_specs=out_specs, check_vma=False
    )
```

```python
import jax
import jax.numpy as jnp
from jax import lax
from jax.experimental import pallas as pl
from jax.experimental.pallas import tpu as pltpu
from jax.sharding import Mesh
from jax.sharding import PartitionSpec as P


D = 16384
STEP = 20
SHARD = ("shard_0", "shard_1", "shard_2")
SIDE = 128
TAIL = 8

beta_one = 0.9
beta_two = 0.95
clip_norm = 1.0

F32 = jnp.float32
BF16 = jnp.bfloat16


def kernel_call(body, out_shape, flops, moved, room=16 * 2**20, **options):
    return pl.pallas_call(
        body,
        out_shape=out_shape,
        compiler_params=pltpu.CompilerParams(vmem_limit_bytes=room),
        cost_estimate=pl.CostEstimate(flops=flops, bytes_accessed=moved, transcendentals=0),
        **options,
    )


def shape(dims, dtype=F32):
    return jax.ShapeDtypeStruct(dims, dtype)


def exchange(x, axes):
    return lax.all_to_all(x, axes, split_axis=0, concat_axis=0, tiled=True)


def turned_column(row):
    return jnp.transpose(jnp.broadcast_to(row, (SIDE, SIDE)))


def stats_body(x, gain, keys, values, key_w, value_w, copies, x_turned, u_turned):
    gain_column = turned_column(gain[...])
    blocks = x.shape[0] // SIDE
    for block in range(blocks):
        rows = pl.ds(block * SIDE, SIDE)
        grad = jnp.dot(keys[rows, :], key_w[...], preferred_element_type=F32)
        grad = grad + jnp.dot(values[rows, :], value_w[...], preferred_element_type=F32)
        x_block = jnp.transpose(x[rows, :].astype(F32))
        u_block = gain_column * jnp.transpose(grad)
        x_turned[:, rows] = x_block.astype(BF16)
        u_turned[:, rows] = u_block
        copies[0, pl.ds(block, 1), :] = jnp.sum(x_block * x_block, axis=0, keepdims=True)
        copies[0, pl.ds(blocks + block, 1), :] = jnp.sum(x_block * u_block, axis=0, keepdims=True)
    own = copies[0]
    for member in range(1, copies.shape[0]):
        copies[member] = own


def spread_body(parts, copies):
    total = parts[0]
    for member in range(1, parts.shape[0]):
        total = total + parts[member]
    copies[...] = jnp.broadcast_to(total[None], copies.shape)


def summed(parts):
    total = parts[0]
    for member in range(1, parts.shape[0]):
        total = total + parts[member]
    return total


def roots(power):
    return 1.0 / jnp.sqrt(power / D + 1e-05)


def gradient_body(
    parts, x_turned, u_turned, gain, keys, values, key_g, value_g, lanes, input_grad, normed
):
    stats = summed(parts)
    blocks = stats.shape[0] // 2
    root = roots(stats[:blocks])
    gain_column = turned_column(gain[...])
    for block in range(blocks):
        rows = pl.ds(block * SIDE, SIDE)
        scaled = x_turned[:, rows].astype(F32) * root[block : block + 1] * gain_column
        normed[:, rows] = scaled.astype(BF16)
    key_g[...] = jnp.dot(normed[...], keys[...], preferred_element_type=F32)
    value_g[...] = jnp.dot(normed[...], values[...], preferred_element_type=F32)
    squares = key_g[...] * key_g[...] + value_g[...] * value_g[...]
    row = jnp.sum(squares, axis=0, keepdims=True)
    total = row[:, :SIDE]
    for start in range(SIDE, row.shape[1], SIDE):
        total = total + row[:, start : start + SIDE]
    lanes[...] = total
    factor = root * root * root * stats[blocks:] / D
    for block in range(blocks):
        rows = pl.ds(block * SIDE, SIDE)
        grad = (
            u_turned[:, rows] * root[block : block + 1]
            - x_turned[:, rows].astype(F32) * factor[block : block + 1]
        )
        input_grad[rows, :] = jnp.transpose(grad).astype(BF16)


def suffix_body(by_section, top, lanes, payload):
    sections, block_rows, width = by_section.shape
    tail = lax.broadcasted_iota(jnp.int32, (TAIL, width), 0)
    whole = lanes[...]
    high = whole.astype(BF16).astype(F32)
    middle = (whole - high).astype(BF16).astype(F32)
    low = whole - high - middle
    pieces = jnp.where(tail == 0, high, 0.0)
    pieces = jnp.where(tail == 1, middle, pieces)
    pieces = jnp.where(tail == 2, low, pieces).astype(BF16)
    running = top[...].astype(F32)
    for section in range(sections - 1, -1, -1):
        running = running + by_section[section].astype(F32)
        payload[section, pl.ds(0, block_rows), :] = running.astype(BF16)
        payload[section, pl.ds(block_rows, TAIL), :] = pieces


def square_spread_body(returned, copies):
    start = returned.shape[1] - TAIL
    pieces = returned[0, pl.ds(start, TAIL), :].astype(F32)
    for member in range(1, returned.shape[0]):
        pieces = pieces + returned[member, pl.ds(start, TAIL), :].astype(F32)
    lanes = jnp.sum(pieces, axis=0, keepdims=True)
    copies[...] = jnp.broadcast_to(lanes[None], copies.shape)


def leaving_body(returned, out):
    block_rows = out.shape[1]
    for owner in range(out.shape[0]):
        out[owner] = returned[owner, pl.ds(0, block_rows), :]


def first_body(key_g, value_g, codes, scale, grads, old, largest):
    for kind, turned in enumerate((key_g, value_g)):
        largest[kind] = jnp.max(jnp.abs(turned[...]), axis=0, keepdims=True)
        for start in range(0, turned.shape[1], SIDE):
            rows = pl.ds(start, SIDE)
            grads[kind, rows, :] = jnp.transpose(turned[:, rows])
            code = codes[kind, rows, :]
            sign_part = jnp.where(code >= 8, -beta_one, beta_one)
            scales = turned_column(scale[kind, :, rows])
            old[kind, rows, :] = scales * sign_part * jnp.exp2(-(code & 7).astype(F32))


def second_body(codes, scale, old):
    for kind in range(codes.shape[0]):
        for start in range(0, codes.shape[1], SIDE):
            rows = pl.ds(start, SIDE)
            scales = turned_column(beta_two * scale[kind, :, rows])
            old[kind, rows, :] = scales * jnp.exp2(-codes[kind, rows, :].astype(F32))


def adam_body(
    parts, grads, first_old, second_old, first_scale, second_scale, largest, way, first, second
):
    total = jnp.sum(summed(parts), axis=1, keepdims=True)
    clip_factor = jnp.minimum(1.0, clip_norm / (jnp.sqrt(total) + 1e-06))
    bias_one = 1.0 - beta_one**STEP
    bias_two = 1.0 - beta_two**STEP
    edge = clip_factor * largest[0]
    first_part = 1.0 / (beta_one * first_scale[0] + (1.0 - beta_one) * edge)
    second_part = 1.0 / (beta_two * second_scale[0] + (1.0 - beta_two) * edge * edge)
    for start in range(0, grads.shape[1], SIDE):
        rows = pl.ds(start, SIDE)
        clipped = clip_factor * grads[0, rows, :]
        first_new = first_old[0, rows, :] + (1.0 - beta_one) * clipped
        second_new = second_old[0, rows, :] + (1.0 - beta_two) * clipped * clipped
        root = jnp.sqrt(second_new * (1.0 / bias_two)) + 1e-08
        way[0, rows, :] = first_new * (1.0 / bias_one) / root
        first[0, rows, :] = first_new * turned_column(first_part[:, start : start + SIDE])
        second[0, rows, :] = second_new * turned_column(second_part[:, start : start + SIDE])


def on_device(
    section_inputs,
    top_grad,
    norm_gain,
    key_grad,
    value_grad,
    key_weight,
    value_weight,
    first_codes,
    second_codes,
    first_scale,
    second_scale,
):
    micro_count, token_count, width = top_grad.shape
    row_count = micro_count * token_count
    features = key_grad.shape[3]
    sections = lax.axis_size("section")
    block_rows = row_count // sections
    stat_rows = 2 * row_count // SIDE
    x = section_inputs[0].reshape(row_count, width)
    keys = key_grad[0].reshape(row_count, features)
    values = value_grad[0].reshape(row_count, features)
    matmul = 2 * row_count * features * width
    slab = 4 * row_count * width
    moments = (2, features, width)
    moment_bytes = 4 * 2 * features * width

    copies, x_turned, u_turned = kernel_call(
        stats_body,
        (
            shape((lax.axis_size(("shard_1", "shard_2")), stat_rows, SIDE)),
            shape((width, row_count), BF16),
            shape((width, row_count)),
        ),
        2 * matmul,
        4 * slab,
        room=60 * 10**6,
    )(x, norm_gain, keys, values, key_weight[0], value_weight[0])
    parts = exchange(copies, ("shard_1", "shard_2"))
    copies = kernel_call(
        spread_body, shape((lax.axis_size("shard_0"), stat_rows, SIDE)), 2**14, 2**17
    )(parts)
    parts = exchange(copies, "shard_0")

    key_g, value_g, lanes, input_grad = kernel_call(
        gradient_body,
        (
            shape((width, features)),
            shape((width, features)),
            shape((1, SIDE)),
            shape((row_count, width), BF16),
        ),
        2 * matmul,
        4 * slab,
        scratch_shapes=[pltpu.VMEM((width, row_count), BF16)],
    )(parts, x_turned, u_turned, norm_gain, keys, values)
    by_section = exchange(input_grad.reshape(sections, block_rows, width), "section")
    lanes = lax.psum(lanes, "shard_2")
    lanes = lax.psum(lanes, "shard_1")

    top_rows = lax.dynamic_slice_in_dim(
        top_grad.reshape(row_count, width), lax.axis_index("section") * block_rows, block_rows
    )
    payload = kernel_call(
        suffix_body, shape((sections, block_rows + TAIL, width), BF16), slab, slab
    )(by_section, top_rows, lanes)
    returned = exchange(payload, "section")
    copies = kernel_call(
        square_spread_body, shape((lax.axis_size("shard_0"), 1, SIDE)), 2**14, 2**17
    )(returned)
    squares = exchange(copies, "shard_0")
    leaving = kernel_call(
        leaving_body, shape((sections, block_rows, width), BF16), slab, slab
    )(returned).reshape(1, micro_count, token_count, width)

    scale_rows = (2, 1, features)
    first_scales = first_scale.reshape(scale_rows)
    second_scales = second_scale.reshape(scale_rows)
    grads, first_old, largest = kernel_call(
        first_body,
        (shape(moments), shape(moments), shape(scale_rows)),
        moment_bytes,
        4 * moment_bytes,
    )(key_g, value_g, first_codes[0], first_scales)
    second_old = kernel_call(
        second_body, shape(moments), moment_bytes, 2 * moment_bytes
    )(second_codes[0], second_scales)

    whole = pl.BlockSpec(squares.shape, lambda kind: (0, 0, 0))
    one = pl.BlockSpec((1,) + moments[1:], lambda kind: (kind, 0, 0))
    row = pl.BlockSpec((1,) + scale_rows[1:], lambda kind: (kind, 0, 0))
    outputs = kernel_call(
        adam_body,
        (shape(moments),) * 3,
        20 * moment_bytes,
        6 * moment_bytes,
        grid=(2,),
        in_specs=[whole] + [one] * 3 + [row] * 3,
        out_specs=[one] * 3,
    )(squares, grads, first_old, second_old, first_scales, second_scales, largest)
    direction, first_ratio, second_ratio = outputs
    return (direction[None], first_ratio[None], second_ratio[None], leaving)


def solution(mesh):
    finer = Mesh(
        mesh.devices.reshape(mesh.shape["section"], 16, 4, 2),
        ("section", "shard_0", "shard_1", "shard_2"),
    )
    in_specs = (
        P("section", None, None, SHARD),
        P(None, None, SHARD),
        P("section", SHARD),
        P("section", None, None, None),
        P("section", None, None, None),
        P("section", None, SHARD),
        P("section", None, SHARD),
        P("section", None, None, SHARD),
        P("section", None, None, SHARD),
        P("section", None, None, SHARD),
        P("section", None, None, SHARD),
    )
    out_specs = (
        P("section", None, None, SHARD),
        P("section", None, None, SHARD),
        P("section", None, None, SHARD),
        P("section", None, None, SHARD),
    )
    return jax.shard_map(
        on_device, mesh=finer, in_specs=in_specs, out_specs=out_specs, check_vma=False
    )
```

```python
import jax
import jax.numpy as jnp
from jax import lax
from jax.experimental import pallas as pl
from jax.experimental.pallas import tpu as pltpu
from jax.sharding import Mesh
from jax.sharding import PartitionSpec as P


D = 16384
STEP = 20
SHARD = ("shard_0", "shard_1", "shard_2")
SIDE = 128

beta_one = 0.9
beta_two = 0.95
clip_norm = 1.0

F32 = jnp.float32
BF16 = jnp.bfloat16


def kernel_call(body, out_shape, flops, moved, room=16 * 2**20, **options):
    return pl.pallas_call(
        body,
        out_shape=out_shape,
        compiler_params=pltpu.CompilerParams(vmem_limit_bytes=room),
        cost_estimate=pl.CostEstimate(flops=flops, bytes_accessed=moved, transcendentals=0),
        **options,
    )


def shape(dims, dtype=F32):
    return jax.ShapeDtypeStruct(dims, dtype)


def exchange(x, axes):
    return lax.all_to_all(x, axes, split_axis=0, concat_axis=0, tiled=True)


def gathered(x, axis):
    return lax.all_gather(x, axis, axis=0, tiled=True)


def turned_column(row):
    return jnp.transpose(jnp.broadcast_to(row, (SIDE, SIDE)))


def stats_body(x, gain, keys, values, key_w, value_w, copies, x_turned, u_turned):
    gain_column = turned_column(gain[...])
    blocks = x.shape[0] // SIDE
    for block in range(blocks):
        rows = pl.ds(block * SIDE, SIDE)
        grad = jnp.dot(keys[rows, :], key_w[...], preferred_element_type=F32)
        grad = grad + jnp.dot(values[rows, :], value_w[...], preferred_element_type=F32)
        x_block = jnp.transpose(x[rows, :].astype(F32))
        u_block = gain_column * jnp.transpose(grad)
        x_turned[:, rows] = x_block.astype(BF16)
        u_turned[:, rows] = u_block
        copies[0, pl.ds(block, 1), :] = jnp.sum(x_block * x_block, axis=0, keepdims=True)
        copies[0, pl.ds(blocks + block, 1), :] = jnp.sum(x_block * u_block, axis=0, keepdims=True)
    own = copies[0]
    for member in range(1, copies.shape[0]):
        copies[member] = own


def sum_body(parts, out):
    out[0] = summed(parts)


def summed(parts):
    total = parts[0]
    for member in range(1, parts.shape[0]):
        total = total + parts[member]
    return total


def roots(power):
    return 1.0 / jnp.sqrt(power / D + 1e-05)


def gradient_body(
    parts, x_turned, u_turned, gain, keys, values, key_g, value_g, lanes, input_grad, normed
):
    stats = summed(parts)
    blocks = stats.shape[0] // 2
    root = roots(stats[:blocks])
    gain_column = turned_column(gain[...])
    for block in range(blocks):
        rows = pl.ds(block * SIDE, SIDE)
        scaled = x_turned[:, rows].astype(F32) * root[block : block + 1] * gain_column
        normed[:, rows] = scaled.astype(BF16)
    key_g[...] = jnp.dot(normed[...], keys[...], preferred_element_type=F32)
    value_g[...] = jnp.dot(normed[...], values[...], preferred_element_type=F32)
    squares = key_g[...] * key_g[...] + value_g[...] * value_g[...]
    row = jnp.sum(squares, axis=0, keepdims=True)
    total = row[:, :SIDE]
    for start in range(SIDE, row.shape[1], SIDE):
        total = total + row[:, start : start + SIDE]
    lanes[0] = total
    factor = root * root * root * stats[blocks:] / D
    for block in range(blocks):
        rows = pl.ds(block * SIDE, SIDE)
        grad = (
            u_turned[:, rows] * root[block : block + 1]
            - x_turned[:, rows].astype(F32) * factor[block : block + 1]
        )
        input_grad[rows, :] = jnp.transpose(grad).astype(BF16)


def suffix_body(by_section, top, out):
    running = top[...].astype(F32)
    for section in range(by_section.shape[0] - 1, -1, -1):
        running = running + by_section[section].astype(F32)
        out[section] = running.astype(BF16)


def total_body(parts, out):
    out[...] = jnp.sum(summed(parts), axis=0, keepdims=True)[None]


def first_body(key_g, value_g, codes, scale, grads, old, largest):
    for kind, turned in enumerate((key_g, value_g)):
        largest[kind] = jnp.max(jnp.abs(turned[...]), axis=0, keepdims=True)
        for start in range(0, turned.shape[1], SIDE):
            rows = pl.ds(start, SIDE)
            grads[kind, rows, :] = jnp.transpose(turned[:, rows])
            code = codes[kind, rows, :]
            sign_part = jnp.where(code >= 8, -beta_one, beta_one)
            scales = turned_column(scale[kind, :, rows])
            old[kind, rows, :] = scales * sign_part * jnp.exp2(-(code & 7).astype(F32))


def second_body(codes, scale, old):
    for kind in range(codes.shape[0]):
        for start in range(0, codes.shape[1], SIDE):
            rows = pl.ds(start, SIDE)
            scales = turned_column(beta_two * scale[kind, :, rows])
            old[kind, rows, :] = scales * jnp.exp2(-codes[kind, rows, :].astype(F32))


def adam_body(
    parts, grads, first_old, second_old, first_scale, second_scale, largest, way, first, second
):
    total = jnp.sum(summed(parts), axis=0, keepdims=True)
    total = jnp.sum(total, axis=1, keepdims=True)
    clip_factor = jnp.minimum(1.0, clip_norm / (jnp.sqrt(total) + 1e-06))
    bias_one = 1.0 - beta_one**STEP
    bias_two = 1.0 - beta_two**STEP
    edge = clip_factor * largest[0]
    first_part = 1.0 / (beta_one * first_scale[0] + (1.0 - beta_one) * edge)
    second_part = 1.0 / (beta_two * second_scale[0] + (1.0 - beta_two) * edge * edge)
    for start in range(0, grads.shape[1], SIDE):
        rows = pl.ds(start, SIDE)
        clipped = clip_factor * grads[0, rows, :]
        first_new = first_old[0, rows, :] + (1.0 - beta_one) * clipped
        second_new = second_old[0, rows, :] + (1.0 - beta_two) * clipped * clipped
        root = jnp.sqrt(second_new * (1.0 / bias_two)) + 1e-08
        way[0, rows, :] = first_new * (1.0 / bias_one) / root
        first[0, rows, :] = first_new * turned_column(first_part[:, start : start + SIDE])
        second[0, rows, :] = second_new * turned_column(second_part[:, start : start + SIDE])


def on_device(
    section_inputs,
    top_grad,
    norm_gain,
    key_grad,
    value_grad,
    key_weight,
    value_weight,
    first_codes,
    second_codes,
    first_scale,
    second_scale,
):
    micro_count, token_count, width = top_grad.shape
    row_count = micro_count * token_count
    features = key_grad.shape[3]
    sections = lax.axis_size("section")
    block_rows = row_count // sections
    stat_rows = 2 * row_count // SIDE
    x = section_inputs[0].reshape(row_count, width)
    keys = key_grad[0].reshape(row_count, features)
    values = value_grad[0].reshape(row_count, features)
    matmul = 2 * row_count * features * width
    slab = 4 * row_count * width
    moments = (2, features, width)
    moment_bytes = 4 * 2 * features * width

    copies, x_turned, u_turned = kernel_call(
        stats_body,
        (
            shape((lax.axis_size(("shard_1", "shard_2")), stat_rows, SIDE)),
            shape((width, row_count), BF16),
            shape((width, row_count)),
        ),
        2 * matmul,
        4 * slab,
        room=60 * 10**6,
    )(x, norm_gain, keys, values, key_weight[0], value_weight[0])
    parts = exchange(copies, ("shard_1", "shard_2"))
    stats = kernel_call(sum_body, shape((1, stat_rows, SIDE)), 2**14, 2**17)(parts)
    parts = gathered(stats, "shard_0")

    key_g, value_g, lanes, input_grad = kernel_call(
        gradient_body,
        (
            shape((width, features)),
            shape((width, features)),
            shape((1, 1, SIDE)),
            shape((row_count, width), BF16),
        ),
        2 * matmul,
        4 * slab,
        scratch_shapes=[pltpu.VMEM((width, row_count), BF16)],
    )(parts, x_turned, u_turned, norm_gain, keys, values)
    squares = gathered(lanes, "section")
    by_section = exchange(input_grad.reshape(sections, block_rows, width), "section")
    squares = gathered(squares.reshape(1, sections, SIDE), "shard_0")

    top_rows = lax.dynamic_slice_in_dim(
        top_grad.reshape(row_count, width), lax.axis_index("section") * block_rows, block_rows
    )
    suffix = kernel_call(
        suffix_body, shape((sections, block_rows, width), BF16), slab, slab
    )(by_section, top_rows)
    returned = exchange(suffix, "section")
    leaving = returned.reshape(1, micro_count, token_count, width)
    lanes = kernel_call(total_body, shape((1, 1, SIDE)), 2**14, 2**17)(squares)
    squares = gathered(lanes, "shard_1")
    squares = gathered(squares.reshape(1, lax.axis_size("shard_1"), SIDE), "shard_2")

    scale_rows = (2, 1, features)
    first_scales = first_scale.reshape(scale_rows)
    second_scales = second_scale.reshape(scale_rows)
    grads, first_old, largest = kernel_call(
        first_body,
        (shape(moments), shape(moments), shape(scale_rows)),
        moment_bytes,
        4 * moment_bytes,
    )(key_g, value_g, first_codes[0], first_scales)
    second_old = kernel_call(
        second_body, shape(moments), moment_bytes, 2 * moment_bytes
    )(second_codes[0], second_scales)

    whole = pl.BlockSpec(squares.shape, lambda kind: (0, 0, 0))
    one = pl.BlockSpec((1,) + moments[1:], lambda kind: (kind, 0, 0))
    row = pl.BlockSpec((1,) + scale_rows[1:], lambda kind: (kind, 0, 0))
    outputs = kernel_call(
        adam_body,
        (shape(moments),) * 3,
        20 * moment_bytes,
        6 * moment_bytes,
        grid=(2,),
        in_specs=[whole] + [one] * 3 + [row] * 3,
        out_specs=[one] * 3,
    )(squares, grads, first_old, second_old, first_scales, second_scales, largest)
    direction, first_ratio, second_ratio = outputs
    return (direction[None], first_ratio[None], second_ratio[None], leaving)


def solution(mesh):
    finer = Mesh(
        mesh.devices.reshape(mesh.shape["section"], 16, 4, 2),
        ("section", "shard_0", "shard_1", "shard_2"),
    )
    in_specs = (
        P("section", None, None, SHARD),
        P(None, None, SHARD),
        P("section", SHARD),
        P("section", None, None, None),
        P("section", None, None, None),
        P("section", None, SHARD),
        P("section", None, SHARD),
        P("section", None, None, SHARD),
        P("section", None, None, SHARD),
        P("section", None, None, SHARD),
        P("section", None, None, SHARD),
    )
    out_specs = (
        P("section", None, None, SHARD),
        P("section", None, None, SHARD),
        P("section", None, None, SHARD),
        P("section", None, None, SHARD),
    )
    return jax.shard_map(
        on_device, mesh=finer, in_specs=in_specs, out_specs=out_specs, check_vma=False
    )
```

```python
import jax
import jax.numpy as jnp
from jax import lax
from jax.experimental import pallas as pl
from jax.experimental.pallas import tpu as pltpu
from jax.sharding import Mesh
from jax.sharding import PartitionSpec as P


D = 16384
STEP = 20
SHARD = ("shard_0", "shard_1", "shard_2")
SIDE = 128
TAIL = 8

beta_one = 0.9
beta_two = 0.95
clip_norm = 1.0

F32 = jnp.float32
BF16 = jnp.bfloat16


def kernel_call(body, out_shape, flops, moved, room=16 * 2**20, **options):
    return pl.pallas_call(
        body,
        out_shape=out_shape,
        compiler_params=pltpu.CompilerParams(vmem_limit_bytes=room),
        cost_estimate=pl.CostEstimate(flops=flops, bytes_accessed=moved, transcendentals=0),
        **options,
    )


def shape(dims, dtype=F32):
    return jax.ShapeDtypeStruct(dims, dtype)


def exchange(x, axes):
    return lax.all_to_all(x, axes, split_axis=0, concat_axis=0, tiled=True)


def turned_column(row):
    return jnp.transpose(jnp.broadcast_to(row, (SIDE, SIDE)))


def split(row):
    tail = lax.broadcasted_iota(jnp.int32, (TAIL, row.shape[1]), 0)
    high = row.astype(BF16).astype(F32)
    middle = (row - high).astype(BF16).astype(F32)
    pieces = jnp.where(tail == 0, high, 0.0)
    pieces = jnp.where(tail == 1, middle, pieces)
    return jnp.where(tail == 2, row - high - middle, pieces).astype(BF16)


def joined(pieces):
    return jnp.sum(pieces.astype(F32), axis=0, keepdims=True)


def stats_body(x, gain, keys, values, key_w, value_w, copies, x_turned, u_turned):
    width = u_turned.shape[0]
    x_turned[pl.ds(width, TAIL), pl.ds(0, width)] = split(gain[...])
    gain_column = turned_column(gain[...])
    blocks = x.shape[0] // SIDE
    for block in range(blocks):
        rows = pl.ds(block * SIDE, SIDE)
        grad = jnp.dot(keys[rows, :], key_w[...], preferred_element_type=F32)
        grad = grad + jnp.dot(values[rows, :], value_w[...], preferred_element_type=F32)
        x_block = jnp.transpose(x[rows, :].astype(F32))
        u_block = gain_column * jnp.transpose(grad)
        x_turned[pl.ds(0, width), rows] = x_block.astype(BF16)
        u_turned[:, rows] = u_block
        copies[0, pl.ds(block, 1), :] = jnp.sum(x_block * x_block, axis=0, keepdims=True)
        copies[0, pl.ds(blocks + block, 1), :] = jnp.sum(x_block * u_block, axis=0, keepdims=True)
    own = copies[0]
    for member in range(1, copies.shape[0]):
        copies[member] = own


def spread_body(parts, copies, rows):
    total = summed(parts)
    blocks = total.shape[0] // 2
    power = total[:blocks]
    high = power.astype(BF16).astype(F32)
    middle = (power - high).astype(BF16).astype(F32)
    for piece, value in enumerate((high, middle, power - high - middle, total[blocks:])):
        rows[pl.ds(piece * blocks, blocks), :] = value
    copies[...] = jnp.broadcast_to(rows[...].astype(BF16)[None], copies.shape)


def power_and_dot(parts):
    stats = summed(parts)
    blocks = stats.shape[0] // 4
    power = stats[:blocks] + stats[blocks : 2 * blocks] + stats[2 * blocks : 3 * blocks]
    return power, stats[3 * blocks :]


def summed(parts):
    total = parts[0].astype(F32)
    for member in range(1, parts.shape[0]):
        total = total + parts[member].astype(F32)
    return total


def roots(power):
    return 1.0 / jnp.sqrt(power / D + 1e-05)


def gradient_body(
    parts, x_turned, u_turned, keys, values, key_g, value_g, payload, normed
):
    power, row_dot = power_and_dot(parts)
    blocks = power.shape[0]
    root = roots(power)
    features = u_turned.shape[0]
    own = pl.ds(0, features)
    gain_column = turned_column(joined(x_turned[pl.ds(features, TAIL), own]))
    for block in range(blocks):
        rows = pl.ds(block * SIDE, SIDE)
        scaled = x_turned[own, rows].astype(F32) * root[block : block + 1] * gain_column
        normed[:, rows] = scaled.astype(BF16)
    key_g[...] = jnp.dot(normed[...], keys[...], preferred_element_type=F32)
    value_g[...] = jnp.dot(normed[...], values[...], preferred_element_type=F32)
    squares = key_g[...] * key_g[...] + value_g[...] * value_g[...]
    row = jnp.sum(squares, axis=0, keepdims=True)
    lanes = row[:, :SIDE]
    for start in range(SIDE, row.shape[1], SIDE):
        lanes = lanes + row[:, start : start + SIDE]
    factor = root * root * root * row_dot / D
    sections, padded_rows, _ = payload.shape
    block_rows = padded_rows - TAIL
    for block in range(blocks):
        rows = pl.ds(block * SIDE, SIDE)
        grad = (
            u_turned[:, rows] * root[block : block + 1]
            - x_turned[own, rows].astype(F32) * factor[block : block + 1]
        )
        grad = jnp.transpose(grad).astype(BF16)
        done = 0
        while done < SIDE:
            section, offset = divmod(block * SIDE + done, block_rows)
            count = min(SIDE - done, block_rows - offset)
            payload[section, pl.ds(offset, count), :] = grad[done : done + count]
            done += count
    pieces = split(lanes)
    for section in range(sections):
        payload[section, pl.ds(block_rows, TAIL), :] = pieces


def suffix_body(received, top, out, lanes):
    block_rows = top.shape[0]
    tail = pl.ds(block_rows, TAIL)
    running = top[...].astype(F32)
    pieces = jnp.zeros((TAIL, top.shape[1]), F32)
    for section in range(received.shape[0] - 1, -1, -1):
        running = running + received[section, pl.ds(0, block_rows), :].astype(F32)
        out[section] = running.astype(BF16)
        pieces = pieces + received[section, tail, :].astype(F32)
    lanes[...] = jnp.sum(pieces, axis=0, keepdims=True)


def leaving_body(returned, out):
    out[...] = returned[...]


def first_body(key_g, value_g, codes, scale, grads, old, largest):
    for kind, turned in enumerate((key_g, value_g)):
        largest[kind] = jnp.max(jnp.abs(turned[...]), axis=0, keepdims=True)
        for start in range(0, turned.shape[1], SIDE):
            rows = pl.ds(start, SIDE)
            grads[kind, rows, :] = jnp.transpose(turned[:, rows])
            code = codes[kind, rows, :]
            sign_part = jnp.where(code >= 8, -beta_one, beta_one)
            scales = turned_column(scale[kind, :, rows])
            old[kind, rows, :] = scales * sign_part * jnp.exp2(-(code & 7).astype(F32))


def second_body(codes, scale, old):
    for kind in range(codes.shape[0]):
        for start in range(0, codes.shape[1], SIDE):
            rows = pl.ds(start, SIDE)
            scales = turned_column(beta_two * scale[kind, :, rows])
            old[kind, rows, :] = scales * jnp.exp2(-codes[kind, rows, :].astype(F32))


def adam_body(
    parts, grads, first_old, second_old, first_scale, second_scale, largest, way, first, second
):
    total = jnp.sum(summed(parts), axis=1, keepdims=True)
    clip_factor = jnp.minimum(1.0, clip_norm / (jnp.sqrt(total) + 1e-06))
    bias_one = 1.0 - beta_one**STEP
    bias_two = 1.0 - beta_two**STEP
    edge = clip_factor * largest[0]
    first_part = 1.0 / (beta_one * first_scale[0] + (1.0 - beta_one) * edge)
    second_part = 1.0 / (beta_two * second_scale[0] + (1.0 - beta_two) * edge * edge)
    for start in range(0, grads.shape[1], SIDE):
        rows = pl.ds(start, SIDE)
        clipped = clip_factor * grads[0, rows, :]
        first_new = first_old[0, rows, :] + (1.0 - beta_one) * clipped
        second_new = second_old[0, rows, :] + (1.0 - beta_two) * clipped * clipped
        root = jnp.sqrt(second_new * (1.0 / bias_two)) + 1e-08
        way[0, rows, :] = first_new * (1.0 / bias_one) / root
        first[0, rows, :] = first_new * turned_column(first_part[:, start : start + SIDE])
        second[0, rows, :] = second_new * turned_column(second_part[:, start : start + SIDE])


def on_device(
    section_inputs,
    top_grad,
    norm_gain,
    key_grad,
    value_grad,
    key_weight,
    value_weight,
    first_codes,
    second_codes,
    first_scale,
    second_scale,
):
    micro_count, token_count, width = top_grad.shape
    row_count = micro_count * token_count
    features = key_grad.shape[3]
    sections = lax.axis_size("section")
    block_rows = row_count // sections
    stat_rows = 2 * row_count // SIDE
    x = section_inputs[0].reshape(row_count, width)
    keys = key_grad[0].reshape(row_count, features)
    values = value_grad[0].reshape(row_count, features)
    matmul = 2 * row_count * features * width
    slab = 4 * row_count * width
    moments = (2, features, width)
    moment_bytes = 4 * 2 * features * width

    copies, x_turned, u_turned = kernel_call(
        stats_body,
        (
            shape((lax.axis_size(("shard_1", "shard_2")), stat_rows, SIDE)),
            shape((width + TAIL, row_count), BF16),
            shape((width, row_count)),
        ),
        2 * matmul,
        4 * slab,
        room=60 * 10**6,
    )(x, norm_gain, keys, values, key_weight[0], value_weight[0])
    parts = exchange(copies, ("shard_1", "shard_2"))
    copies = kernel_call(
        spread_body,
        shape((lax.axis_size("shard_0"), 2 * stat_rows, SIDE), BF16),
        2**14,
        2**17,
        scratch_shapes=[pltpu.VMEM((2 * stat_rows, SIDE), F32)],
    )(parts)
    parts = exchange(copies, "shard_0")

    key_g, value_g, payload = kernel_call(
        gradient_body,
        (
            shape((width, features)),
            shape((width, features)),
            shape((sections, block_rows + TAIL, width), BF16),
        ),
        2 * matmul,
        4 * slab,
        scratch_shapes=[pltpu.VMEM((width, row_count), BF16)],
    )(parts, x_turned, u_turned, keys, values)
    received = exchange(payload, "section")
    top_rows = lax.dynamic_slice_in_dim(
        top_grad.reshape(row_count, width), lax.axis_index("section") * block_rows, block_rows
    )
    suffix, lanes = kernel_call(
        suffix_body, (shape((sections, block_rows, width), BF16), shape((1, SIDE))), slab, slab
    )(received, top_rows)
    returned = exchange(suffix, "section")
    lanes = lax.psum(lanes, "shard_2")
    lanes = lax.psum(lanes, "shard_1")
    copies = jnp.broadcast_to(lanes[None], (lax.axis_size("shard_0"), 1, SIDE))
    squares = exchange(copies, "shard_0")
    leaving = kernel_call(
        leaving_body, shape((row_count, width), BF16), slab, slab
    )(returned.reshape(row_count, width)).reshape(1, micro_count, token_count, width)

    scale_rows = (2, 1, features)
    first_scales = first_scale.reshape(scale_rows)
    second_scales = second_scale.reshape(scale_rows)
    grads, first_old, largest = kernel_call(
        first_body,
        (shape(moments), shape(moments), shape(scale_rows)),
        moment_bytes,
        4 * moment_bytes,
    )(key_g, value_g, first_codes[0], first_scales)
    second_old = kernel_call(
        second_body, shape(moments), moment_bytes, 2 * moment_bytes
    )(second_codes[0], second_scales)

    whole = pl.BlockSpec(squares.shape, lambda kind: (0, 0, 0))
    one = pl.BlockSpec((1,) + moments[1:], lambda kind: (kind, 0, 0))
    row = pl.BlockSpec((1,) + scale_rows[1:], lambda kind: (kind, 0, 0))
    outputs = kernel_call(
        adam_body,
        (shape(moments),) * 3,
        20 * moment_bytes,
        6 * moment_bytes,
        grid=(2,),
        in_specs=[whole] + [one] * 3 + [row] * 3,
        out_specs=[one] * 3,
    )(squares, grads, first_old, second_old, first_scales, second_scales, largest)
    direction, first_ratio, second_ratio = outputs
    return (direction[None], first_ratio[None], second_ratio[None], leaving)


def solution(mesh):
    finer = Mesh(
        mesh.devices.reshape(mesh.shape["section"], 16, 4, 2),
        ("section", "shard_0", "shard_1", "shard_2"),
    )
    in_specs = (
        P("section", None, None, SHARD),
        P(None, None, SHARD),
        P("section", SHARD),
        P("section", None, None, None),
        P("section", None, None, None),
        P("section", None, SHARD),
        P("section", None, SHARD),
        P("section", None, None, SHARD),
        P("section", None, None, SHARD),
        P("section", None, None, SHARD),
        P("section", None, None, SHARD),
    )
    out_specs = (
        P("section", None, None, SHARD),
        P("section", None, None, SHARD),
        P("section", None, None, SHARD),
        P("section", None, None, SHARD),
    )
    return jax.shard_map(
        on_device, mesh=finer, in_specs=in_specs, out_specs=out_specs, check_vma=False
    )
```

```python
import jax
import jax.numpy as jnp
from jax import lax
from jax.experimental import pallas as pl
from jax.experimental.pallas import tpu as pltpu
from jax.sharding import Mesh
from jax.sharding import PartitionSpec as P


D = 16384
STEP = 20
SHARD = ("shard_0", "shard_1", "shard_2")
SIDE = 128
TAIL = 8

beta_one = 0.9
beta_two = 0.95
clip_norm = 1.0

F32 = jnp.float32
BF16 = jnp.bfloat16


def kernel_call(body, out_shape, flops, moved, room=16 * 2**20, **options):
    return pl.pallas_call(
        body,
        out_shape=out_shape,
        compiler_params=pltpu.CompilerParams(vmem_limit_bytes=room),
        cost_estimate=pl.CostEstimate(flops=flops, bytes_accessed=moved, transcendentals=0),
        **options,
    )


def shape(dims, dtype=F32):
    return jax.ShapeDtypeStruct(dims, dtype)


def exchange(x, axes):
    return lax.all_to_all(x, axes, split_axis=0, concat_axis=0, tiled=True)


def turned_column(row):
    return jnp.transpose(jnp.broadcast_to(row, (SIDE, SIDE)))


def split(row):
    tail = lax.broadcasted_iota(jnp.int32, (TAIL, row.shape[1]), 0)
    high = row.astype(BF16).astype(F32)
    middle = (row - high).astype(BF16).astype(F32)
    pieces = jnp.where(tail == 0, high, 0.0)
    pieces = jnp.where(tail == 1, middle, pieces)
    return jnp.where(tail == 2, row - high - middle, pieces).astype(BF16)


def joined(pieces):
    return jnp.sum(pieces.astype(F32), axis=0, keepdims=True)


def stats_body(x, gain, keys, values, key_w, value_w, copies, x_turned, u_turned):
    width = u_turned.shape[0]
    x_turned[pl.ds(width, TAIL), pl.ds(0, width)] = split(gain[...])
    gain_column = turned_column(gain[...])
    blocks = x.shape[0] // SIDE
    for block in range(blocks):
        rows = pl.ds(block * SIDE, SIDE)
        grad = jnp.dot(keys[rows, :], key_w[...], preferred_element_type=F32)
        grad = grad + jnp.dot(values[rows, :], value_w[...], preferred_element_type=F32)
        x_block = jnp.transpose(x[rows, :].astype(F32))
        u_block = gain_column * jnp.transpose(grad)
        x_turned[pl.ds(0, width), rows] = x_block.astype(BF16)
        u_turned[:, rows] = u_block
        copies[0, pl.ds(block, 1), :] = jnp.sum(x_block * x_block, axis=0, keepdims=True)
        copies[0, pl.ds(blocks + block, 1), :] = jnp.sum(x_block * u_block, axis=0, keepdims=True)
    own = copies[0]
    for member in range(1, copies.shape[0]):
        copies[member] = own


def spread_body(parts, copies, rows):
    total = summed(parts)
    blocks = total.shape[0] // 2
    power = total[:blocks]
    high = power.astype(BF16).astype(F32)
    middle = (power - high).astype(BF16).astype(F32)
    for piece, value in enumerate((high, middle, power - high - middle, total[blocks:])):
        rows[pl.ds(piece * blocks, blocks), :] = value
    copies[...] = jnp.broadcast_to(rows[...].astype(BF16)[None], copies.shape)


def power_and_dot(parts):
    stats = summed(parts)
    blocks = stats.shape[0] // 4
    power = stats[:blocks] + stats[blocks : 2 * blocks] + stats[2 * blocks : 3 * blocks]
    return power, stats[3 * blocks :]


def summed(parts):
    total = parts[0].astype(F32)
    for member in range(1, parts.shape[0]):
        total = total + parts[member].astype(F32)
    return total


def roots(power):
    return 1.0 / jnp.sqrt(power / D + 1e-05)


def gradient_body(
    parts, x_turned, u_turned, keys, values, key_g, value_g, payload, normed
):
    power, row_dot = power_and_dot(parts)
    blocks = power.shape[0]
    root = roots(power)
    features = u_turned.shape[0]
    own = pl.ds(0, features)
    gain_column = turned_column(joined(x_turned[pl.ds(features, TAIL), own]))
    for block in range(blocks):
        rows = pl.ds(block * SIDE, SIDE)
        scaled = x_turned[own, rows].astype(F32) * root[block : block + 1] * gain_column
        normed[:, rows] = scaled.astype(BF16)
    key_g[...] = jnp.dot(normed[...], keys[...], preferred_element_type=F32)
    value_g[...] = jnp.dot(normed[...], values[...], preferred_element_type=F32)
    squares = key_g[...] * key_g[...] + value_g[...] * value_g[...]
    row = jnp.sum(squares, axis=0, keepdims=True)
    lanes = row[:, :SIDE]
    for start in range(SIDE, row.shape[1], SIDE):
        lanes = lanes + row[:, start : start + SIDE]
    factor = root * root * root * row_dot / D
    sections, padded_rows, _ = payload.shape
    block_rows = padded_rows - TAIL
    for block in range(blocks):
        rows = pl.ds(block * SIDE, SIDE)
        grad = (
            u_turned[:, rows] * root[block : block + 1]
            - x_turned[own, rows].astype(F32) * factor[block : block + 1]
        )
        grad = jnp.transpose(grad).astype(BF16)
        done = 0
        while done < SIDE:
            section, offset = divmod(block * SIDE + done, block_rows)
            count = min(SIDE - done, block_rows - offset)
            payload[section, pl.ds(offset, count), :] = grad[done : done + count]
            done += count
    pieces = split(lanes)
    for section in range(sections):
        payload[section, pl.ds(block_rows, TAIL), :] = pieces


def suffix_body(received, top, out, lanes):
    block_rows = top.shape[0]
    tail = pl.ds(block_rows, TAIL)
    running = top[...].astype(F32)
    pieces = jnp.zeros((TAIL, top.shape[1]), F32)
    for section in range(received.shape[0] - 1, -1, -1):
        running = running + received[section, pl.ds(0, block_rows), :].astype(F32)
        out[section] = running.astype(BF16)
        pieces = pieces + received[section, tail, :].astype(F32)
    lanes[...] = jnp.broadcast_to(jnp.sum(pieces, axis=0, keepdims=True)[None], lanes.shape)


def leaving_body(returned, out):
    out[...] = returned[...]


def first_body(key_g, value_g, codes, scale, grads, old, largest):
    for kind, turned in enumerate((key_g, value_g)):
        largest[kind] = jnp.max(jnp.abs(turned[...]), axis=0, keepdims=True)
        for start in range(0, turned.shape[1], SIDE):
            rows = pl.ds(start, SIDE)
            grads[kind, rows, :] = jnp.transpose(turned[:, rows])
            code = codes[kind, rows, :]
            sign_part = jnp.where(code >= 8, -beta_one, beta_one)
            scales = turned_column(scale[kind, :, rows])
            old[kind, rows, :] = scales * sign_part * jnp.exp2(-(code & 7).astype(F32))


def second_body(codes, scale, old):
    for kind in range(codes.shape[0]):
        for start in range(0, codes.shape[1], SIDE):
            rows = pl.ds(start, SIDE)
            scales = turned_column(beta_two * scale[kind, :, rows])
            old[kind, rows, :] = scales * jnp.exp2(-codes[kind, rows, :].astype(F32))


def adam_body(
    parts, grads, first_old, second_old, first_scale, second_scale, largest, way, first, second
):
    total = jnp.sum(summed(parts), axis=1, keepdims=True)
    clip_factor = jnp.minimum(1.0, clip_norm / (jnp.sqrt(total) + 1e-06))
    bias_one = 1.0 - beta_one**STEP
    bias_two = 1.0 - beta_two**STEP
    edge = clip_factor * largest[0]
    first_part = 1.0 / (beta_one * first_scale[0] + (1.0 - beta_one) * edge)
    second_part = 1.0 / (beta_two * second_scale[0] + (1.0 - beta_two) * edge * edge)
    for start in range(0, grads.shape[1], SIDE):
        rows = pl.ds(start, SIDE)
        clipped = clip_factor * grads[0, rows, :]
        first_new = first_old[0, rows, :] + (1.0 - beta_one) * clipped
        second_new = second_old[0, rows, :] + (1.0 - beta_two) * clipped * clipped
        root = jnp.sqrt(second_new * (1.0 / bias_two)) + 1e-08
        way[0, rows, :] = first_new * (1.0 / bias_one) / root
        first[0, rows, :] = first_new * turned_column(first_part[:, start : start + SIDE])
        second[0, rows, :] = second_new * turned_column(second_part[:, start : start + SIDE])


def on_device(
    section_inputs,
    top_grad,
    norm_gain,
    key_grad,
    value_grad,
    key_weight,
    value_weight,
    first_codes,
    second_codes,
    first_scale,
    second_scale,
):
    micro_count, token_count, width = top_grad.shape
    row_count = micro_count * token_count
    features = key_grad.shape[3]
    sections = lax.axis_size("section")
    block_rows = row_count // sections
    stat_rows = 2 * row_count // SIDE
    x = section_inputs[0].reshape(row_count, width)
    keys = key_grad[0].reshape(row_count, features)
    values = value_grad[0].reshape(row_count, features)
    matmul = 2 * row_count * features * width
    slab = 4 * row_count * width
    moments = (2, features, width)
    moment_bytes = 4 * 2 * features * width

    copies, x_turned, u_turned = kernel_call(
        stats_body,
        (
            shape((lax.axis_size(("shard_1", "shard_2")), stat_rows, SIDE)),
            shape((width + TAIL, row_count), BF16),
            shape((width, row_count)),
        ),
        2 * matmul,
        4 * slab,
        room=60 * 10**6,
    )(x, norm_gain, keys, values, key_weight[0], value_weight[0])
    parts = exchange(copies, ("shard_1", "shard_2"))
    copies = kernel_call(
        spread_body,
        shape((lax.axis_size("shard_0"), 2 * stat_rows, SIDE), BF16),
        2**14,
        2**17,
        scratch_shapes=[pltpu.VMEM((2 * stat_rows, SIDE), F32)],
    )(parts)
    parts = exchange(copies, "shard_0")

    key_g, value_g, payload = kernel_call(
        gradient_body,
        (
            shape((width, features)),
            shape((width, features)),
            shape((sections, block_rows + TAIL, width), BF16),
        ),
        2 * matmul,
        4 * slab,
        scratch_shapes=[pltpu.VMEM((width, row_count), BF16)],
    )(parts, x_turned, u_turned, keys, values)
    received = exchange(payload, "section")
    top_rows = lax.dynamic_slice_in_dim(
        top_grad.reshape(row_count, width), lax.axis_index("section") * block_rows, block_rows
    )
    suffix, lanes = kernel_call(
        suffix_body,
        (shape((sections, block_rows, width), BF16), shape((lax.axis_size("shard_0"), 1, SIDE))),
        slab,
        slab,
    )(received, top_rows)
    returned = exchange(suffix, "section")
    lanes = lax.psum(lanes, "shard_2")
    lanes = lax.psum(lanes, "shard_1")
    squares = exchange(lanes, "shard_0")
    leaving = kernel_call(
        leaving_body, shape((row_count, width), BF16), slab, slab
    )(returned.reshape(row_count, width)).reshape(1, micro_count, token_count, width)

    scale_rows = (2, 1, features)
    first_scales = first_scale.reshape(scale_rows)
    second_scales = second_scale.reshape(scale_rows)
    grads, first_old, largest = kernel_call(
        first_body,
        (shape(moments), shape(moments), shape(scale_rows)),
        moment_bytes,
        4 * moment_bytes,
    )(key_g, value_g, first_codes[0], first_scales)
    second_old = kernel_call(
        second_body, shape(moments), moment_bytes, 2 * moment_bytes
    )(second_codes[0], second_scales)

    whole = pl.BlockSpec(squares.shape, lambda kind, half: (0, 0, 0))
    one = pl.BlockSpec((1, features // 2, width), lambda kind, half: (kind, half, 0))
    row = pl.BlockSpec((1, 1, features // 2), lambda kind, half: (kind, 0, half))
    outputs = kernel_call(
        adam_body,
        (shape(moments),) * 3,
        20 * moment_bytes,
        6 * moment_bytes,
        grid=(2, 2),
        in_specs=[whole] + [one] * 3 + [row] * 3,
        out_specs=[one] * 3,
    )(squares, grads, first_old, second_old, first_scales, second_scales, largest)
    direction, first_ratio, second_ratio = outputs
    return (direction[None], first_ratio[None], second_ratio[None], leaving)


def solution(mesh):
    finer = Mesh(
        mesh.devices.reshape(mesh.shape["section"], 16, 4, 2),
        ("section", "shard_0", "shard_1", "shard_2"),
    )
    in_specs = (
        P("section", None, None, SHARD),
        P(None, None, SHARD),
        P("section", SHARD),
        P("section", None, None, None),
        P("section", None, None, None),
        P("section", None, SHARD),
        P("section", None, SHARD),
        P("section", None, None, SHARD),
        P("section", None, None, SHARD),
        P("section", None, None, SHARD),
        P("section", None, None, SHARD),
    )
    out_specs = (
        P("section", None, None, SHARD),
        P("section", None, None, SHARD),
        P("section", None, None, SHARD),
        P("section", None, None, SHARD),
    )
    return jax.shard_map(
        on_device, mesh=finer, in_specs=in_specs, out_specs=out_specs, check_vma=False
    )
```
